32 devices in a mesh: groups: 1, row: 32 (over z, y, x, core), col: 1.
Axes of the slice: x: 2, y: 2, z: 4, core: 2. Of those that a mesh axis runs over, the one named last changes fastest.
Arguments:
- pair_map: bfloat16 [128, 128, 288], P(('groups', 'col'), 'row'), may hold values from -10 to 10
- row_gain: float32 [288], replicated, may hold values from 0.1 to 1.9
- row_proj: bfloat16 [288, 1152], replicated, may hold values from -0.5 to 0.5
- row_gate_bias: float32 [288], replicated, may hold values from -4 to 4
- row_out: bfloat16 [288, 288], replicated, may hold values from -0.375 to 0.375
- col_gain: float32 [288], replicated, may hold values from 0.1 to 1.9
- col_proj: bfloat16 [288, 1152], replicated, may hold values from -0.5 to 0.5
- col_gate_bias: float32 [288], replicated, may hold values from -4 to 4
- col_out: bfloat16 [288, 288], replicated, may hold values from -0.375 to 0.375
Outputs:
- updated_map: bfloat16 [128, 128, 288], P(('groups', 'col'), 'row')
The draws below stay inside these ranges and needn't reach their ends.
All inputs are finite; a program needn't handle non-finite values.
Results may differ from the reference program's by a relative error of at most 0.006.
Values may be sent and summed in bfloat16 or wider, within the bound.
A program may use at most 64 MiB of HBM per device.

```python
import math
import jax
import jax.numpy as jnp
from jax import lax

WIDTH = 288
HEADS = 8
LENGTH = 128


def drawn_projection(key, salt):
    softmax_weights = jax.random.truncated_normal(jax.random.fold_in(key, salt), -2.5, 2.5, (WIDTH, 4 * WIDTH), jnp.float32)
    softmax_weights = softmax_weights / math.sqrt(WIDTH)
    return softmax_weights


def draw_pair_map(key, part):
    ground = jax.random.truncated_normal(jax.random.fold_in(key, 11), -6.0, 6.0, (LENGTH, LENGTH, WIDTH), jnp.float32)
    return ground.astype(jnp.bfloat16)


def draw_row_proj(key, part):
    return drawn_projection(key, 21).astype(jnp.bfloat16)


def draw_col_proj(key, part):
    return drawn_projection(key, 37).astype(jnp.bfloat16)


def normal_values(key, dims, scale, bound, kind=jnp.bfloat16):
    result = scale * jax.random.normal(key, dims, jnp.float32)
    return jnp.clip(result, min=-bound, max=bound).astype(kind)


def setup_inputs(seed: int = 0, part: int = 0) -> dict:
    seeds = jax.random.split(jax.random.key(seed), 10)
    part_keys = jax.random.split(jax.random.fold_in(seeds[9], part), 10)
    return {
        "pair_map": draw_pair_map(jax.random.fold_in(jax.random.fold_in(seeds[9], part), 71), part),
        "row_gain": jnp.clip(1.0 + 0.18 * jax.random.normal(seeds[1], (WIDTH,), jnp.float32), 0.1, 1.9),
        "row_proj": draw_row_proj(jax.random.fold_in(seeds[9], 71), part),
        "row_gate_bias": normal_values(seeds[3], (WIDTH,), 1.0, 4.0, jnp.float32),
        "row_out": normal_values(seeds[4], (WIDTH, WIDTH), WIDTH ** -0.5, 0.375),
        "col_gain": jnp.clip(1.0 + 0.18 * jax.random.normal(seeds[5], (WIDTH,), jnp.float32), 0.1, 1.9),
        "col_proj": draw_col_proj(jax.random.fold_in(seeds[9], 71), part),
        "col_gate_bias": normal_values(seeds[7], (WIDTH,), 1.0, 4.0, jnp.float32),
        "col_out": normal_values(seeds[8], (WIDTH, WIDTH), WIDTH ** -0.5, 0.375),
    }


def attend_rows(block, gain, w_proj, gate_bias, w_out):
    width = block.shape[-1]
    head_count = HEADS
    per_head_width = width // head_count
    source = block.astype(jnp.float32)
    average = lax.optimization_barrier(jnp.mean(source, -1, keepdims=True))
    centred = source - average
    spread = lax.optimization_barrier(jnp.mean(centred * centred, -1, keepdims=True))
    normed = (centred * lax.rsqrt(spread + 1e-05) * gain).astype(jnp.bfloat16)
    projected = jnp.dot(normed.reshape(-1, width), w_proj, preferred_element_type=jnp.float32)
    projected = projected.reshape(block.shape[:-1] + (4 * width,))
    query_rows = projected[..., :width].astype(jnp.bfloat16).astype(jnp.float32)
    key_rows = projected[..., width:2 * width].astype(jnp.bfloat16).astype(jnp.float32)
    value_rows = projected[..., 2 * width:3 * width].astype(jnp.bfloat16).astype(jnp.float32)
    gating = jax.nn.sigmoid(projected[..., 3 * width:] + gate_bias)
    score_scale_factor = 1.0 / per_head_width ** 0.5
    head_outputs = []
    for head_index in range(head_count):
        lower_start = head_index * per_head_width
        logit_matrix = jnp.einsum('duv,dtv->dut', query_rows[..., lower_start:lower_start + per_head_width], key_rows[..., lower_start:lower_start + per_head_width]) * score_scale_factor
        softmax_weights = jax.nn.softmax(logit_matrix, -1).astype(jnp.bfloat16).astype(jnp.float32)
        head_outputs.append(jnp.einsum('twn,tnl->twl', softmax_weights, value_rows[..., lower_start:lower_start + per_head_width]))
    mixed = jnp.concatenate(head_outputs, -1)
    gated = (mixed * gating).astype(jnp.bfloat16)
    changes = jnp.dot(gated.reshape(-1, width), w_out, preferred_element_type=jnp.float32).reshape(block.shape)
    return (source + changes).astype(jnp.bfloat16)

def axial(pair_map, gain, w_proj, gate_bias, w_out):
    blocks = pair_map.reshape(LENGTH // 16, 16, LENGTH, WIDTH)
    done = lax.map(lambda piece: attend_rows(piece, gain, w_proj, gate_bias, w_out), blocks)
    return done.reshape(LENGTH, LENGTH, WIDTH)

def reference(pair_map, row_gain, row_proj, row_gate_bias, row_out, col_gain, col_proj, col_gate_bias, col_out):
    row_done = axial(pair_map, row_gain, row_proj, row_gate_bias, row_out)
    turned = jnp.transpose(row_done, (1, 0, 2))
    col_done = axial(turned, col_gain, col_proj, col_gate_bias, col_out)
    return jnp.transpose(col_done, (1, 0, 2))
```

```python
import functools
import math

import jax
import jax.numpy as jnp
from jax import lax
from jax.experimental import pallas as pl
from jax.experimental.pallas import tpu as pltpu
from jax.sharding import PartitionSpec as P

HEADS = 8
LANES = 128
F32 = jnp.float32
BF16 = jnp.bfloat16
MESH = pl.DeviceIdType.MESH


def ceil_to(value, step):
    return -(-value // step) * step


def nt(a, b):
    return lax.dot_general(a, b, (((1,), (1,)), ((), ())), preferred_element_type=F32)


def tn(a, b):
    return lax.dot_general(a, b, (((0,), (0,)), ((), ())), preferred_element_type=F32)


def nn(a, b):
    return jnp.dot(a, b, preferred_element_type=F32)


class Sizes:
    def __init__(self, width):
        self.width = width
        self.head = width // HEADS
        self.pad_head = ceil_to(self.head + 1, 16)
        self.rows = HEADS * self.pad_head
        self.lanes = ceil_to(width, LANES)
        self.chunks = self.lanes // LANES

    def weight_scratch(self):
        return [
            pltpu.VMEM((self.width, HEADS * LANES), BF16),
            pltpu.VMEM((self.width, HEADS * LANES), BF16),
            pltpu.VMEM((self.rows, self.width), BF16),
            pltpu.VMEM((self.rows, self.width), BF16),
            pltpu.VMEM((self.rows, self.lanes), BF16),
            pltpu.VMEM((self.rows, 1), F32),
        ]

    def token_scratch(self, tokens):
        return [pltpu.VMEM((self.chunks, tokens, LANES), F32)] * 2


def prepare(sz, weights, packed):
    proj, bias, out = weights
    wq, wk, wvt, wgt, wo, bias_col = packed

    def window(block):
        start = block * sz.width
        low = start // LANES * LANES
        high = min(ceil_to(start + sz.width, LANES), 4 * sz.width)
        return proj[:, low:high], start - low, high - low

    for block, ref in ((0, wq), (1, wk)):
        part, shift, size = window(block)
        source = lax.broadcasted_iota(jnp.int32, (size, HEADS * LANES), 0) - shift
        lane = lax.broadcasted_iota(jnp.int32, (size, HEADS * LANES), 1)
        inner = lane % LANES
        hit = (inner < sz.head) & (source == lane // LANES * sz.head + inner)
        ref[...] = nn(part, jnp.where(hit, 1.0, 0.0).astype(BF16)).astype(BF16)

    def row_hits(size, shift):
        source = lax.broadcasted_iota(jnp.int32, (sz.rows, size), 1) - shift
        row = lax.broadcasted_iota(jnp.int32, (sz.rows, size), 0)
        inner = row % sz.pad_head
        return (inner < sz.head) & (source == row // sz.pad_head * sz.head + inner)

    for block, ref in ((2, wvt), (3, wgt)):
        part, shift, size = window(block)
        pick = jnp.where(row_hits(size, shift), 1.0, 0.0).astype(BF16)
        ref[...] = nt(pick, part).astype(BF16)
    hits = row_hits(sz.width, 0)
    pick = jnp.where(hits, 1.0, 0.0).astype(BF16)
    wo[...] = jnp.zeros_like(wo)
    wo[:, : sz.width] = nn(pick, out[...]).astype(BF16)
    bias_col[...] = jnp.sum(jnp.where(hits, bias[...], 0.0), axis=1, keepdims=True)


def attend(sz, groups, length, start_of, stride, per_group, gain, packed, xs, ys):
    wq, wk, wvt, wgt, wo, bias_col = packed
    run = length // per_group
    factor = math.log2(math.e) / sz.head**0.5
    lane = lax.broadcasted_iota(jnp.int32, (1, sz.lanes), 1)
    inside = lane < sz.width
    feature = lax.broadcasted_iota(jnp.int32, (sz.rows, 1), 0)
    ones_row = jnp.where(feature % sz.pad_head == sz.head, 1.0, 0.0)
    for group in range(groups):
        places = [pl.ds(start_of(group, c), run, stride=stride) for c in range(per_group)]
        x = jnp.concatenate(
            [
                jnp.concatenate([xs[k, place, :] for place in places], axis=0)
                for k in range(sz.chunks)
            ],
            axis=1,
        )
        mean = jnp.sum(x, axis=1, keepdims=True) * (1.0 / sz.width)
        centred = jnp.where(inside, x - mean, 0.0)
        spread = jnp.sum(centred * centred, axis=1, keepdims=True) * (1.0 / sz.width)
        normed = centred[:, : sz.width] * lax.rsqrt(spread + 1e-05) * gain[...]
        normed = normed.astype(BF16)
        q = (nn(normed, wq[...]) * factor).astype(BF16)
        k = nn(normed, wk[...]).astype(BF16)
        vt = (nt(wvt[...], normed) + ones_row).astype(BF16)
        gate = jax.nn.sigmoid(nt(wgt[...], normed) + bias_col[...])
        pieces = []
        for head in range(HEADS):
            lanes = slice(head * LANES, (head + 1) * LANES)
            rows = slice(head * sz.pad_head, (head + 1) * sz.pad_head)
            scores = nt(k[:, lanes], q[:, lanes])
            top = jnp.max(scores, axis=0, keepdims=True)
            weight = jnp.exp2(scores - top).astype(BF16)
            mixed = nn(vt[rows], weight)
            total = mixed[sz.head : sz.head + 1]
            pieces.append((mixed * (1.0 / total) * gate[rows]).astype(BF16))
        gated = jnp.concatenate(pieces, axis=0)
        y = x + tn(gated, wo[...])
        for k_chunk in range(sz.chunks):
            part = y[:, k_chunk * LANES : (k_chunk + 1) * LANES]
            for c, place in enumerate(places):
                ys[k_chunk, place, :] = part[c * run : (c + 1) * run]


def spread_tokens(sz, source, xs):
    tokens = xs.shape[1]
    flat = source[...].astype(F32).reshape(tokens, sz.width)
    for k in range(sz.chunks):
        part = flat[:, k * LANES : min((k + 1) * LANES, sz.width)]
        if part.shape[1] < LANES:
            pad = jnp.zeros((tokens, LANES - part.shape[1]), F32)
            part = jnp.concatenate([part, pad], axis=1)
        xs[k] = part


def gather_tokens(sz, ys, target):
    shape = target.shape
    for k in range(sz.chunks):
        low, high = k * LANES, min((k + 1) * LANES, sz.width)
        part = ys[k][:, : high - low]
        target[..., low:high] = part.reshape(shape[:-1] + (high - low,)).astype(BF16)


def row_kernel(
    sz, n, rows, cols, x_ref, gain, proj, bias, out_w, result, got, back, xs, ys, *rest
):
    packed = rest[:6]
    send_a, recv_a, send_b, recv_b, local_sem = rest[6:]
    me = lax.axis_index("row")

    barrier = pltpu.get_barrier_semaphore()

    def greet(step, carry):
        peer = lax.rem(me + step, n)
        pl.semaphore_signal(barrier, inc=1, device_id={"row": peer}, device_id_type=MESH)
        return carry

    lax.fori_loop(1, n, greet, 0)
    pl.semaphore_wait(barrier, n - 1)

    def copy(source, target, send, recv, peer, slot):
        return pltpu.make_async_remote_copy(
            src_ref=source.at[peer],
            dst_ref=target.at[slot],
            send_sem=send.at[peer],
            recv_sem=recv.at[slot],
            device_id={"row": peer},
            device_id_type=MESH,
        )

    def exchange(source, target, send, recv, work):
        def start(step, carry):
            peer = lax.rem(me + step, n)
            copy(source, target, send, recv, peer, me).start()
            return carry

        lax.fori_loop(1, n, start, 0)
        own = pltpu.make_async_copy(source.at[me], target.at[me], local_sem)
        own.start()
        work()
        own.wait()

        def finish(step, carry):
            peer = lax.rem(me + step, n)
            copy(source, target, send, recv, peer, me).wait_send()
            copy(source, target, send, recv, peer, peer).wait_recv()
            return carry

        lax.fori_loop(1, n, finish, 0)

    exchange(x_ref, got, send_a, recv_a, lambda: prepare(sz, (proj, bias, out_w), packed))
    spread_tokens(sz, got, xs)
    block = rows * cols
    attend(
        sz, rows, n * cols, lambda g, c: g * cols + c, block, cols, gain, packed, xs, ys
    )
    gather_tokens(sz, ys, back)
    exchange(back, result, send_b, recv_b, lambda: None)


def col_kernel(sz, cols, x_ref, gain, proj, bias, out_w, result, xs, ys, *packed):
    prepare(sz, (proj, bias, out_w), packed)
    spread_tokens(sz, x_ref, xs)
    length = xs.shape[1] // cols
    attend(sz, cols, length, lambda g, c: g, cols, 1, gain, packed, xs, ys)
    gather_tokens(sz, ys, result)


VMEM = pl.BlockSpec(memory_space=pltpu.VMEM)


def per_device(
    pair_map, row_gain, row_proj, row_gate_bias, row_out, col_gain, col_proj, col_gate_bias, col_out
):
    local_rows, local_cols, width = pair_map.shape
    n = lax.axis_size("row")
    sz = Sizes(width)
    rows = local_rows // n
    tokens = local_rows * local_cols
    block = rows * local_cols
    shape = (n, block, width)
    done = pl.pallas_call(
        functools.partial(row_kernel, sz, n, rows, local_cols),
        out_shape=jax.ShapeDtypeStruct(shape, BF16),
        in_specs=[VMEM] * 5,
        out_specs=VMEM,
        scratch_shapes=[pltpu.VMEM(shape, BF16)] * 2
        + sz.token_scratch(tokens)
        + sz.weight_scratch()
        + [pltpu.SemaphoreType.DMA((n,))] * 4
        + [pltpu.SemaphoreType.DMA],
        compiler_params=pltpu.CompilerParams(collective_id=0, has_side_effects=True),
        name="row_attention",
    )(
        pair_map.reshape(shape),
        row_gain.reshape(1, width),
        row_proj,
        row_gate_bias.reshape(1, width),
        row_out,
    )
    splits = lax.axis_size("col")
    if splits > 1:
        done = done.reshape(local_rows, local_cols, width)
        done = lax.all_to_all(done, "col", split_axis=1, concat_axis=0, tiled=True)
    cols = local_cols // splits
    full = tokens // cols
    updated = pl.pallas_call(
        functools.partial(col_kernel, sz, cols),
        out_shape=jax.ShapeDtypeStruct(shape, BF16),
        in_specs=[VMEM] * 5,
        out_specs=VMEM,
        scratch_shapes=sz.token_scratch(tokens) + sz.weight_scratch(),
        name="col_attention",
    )(
        done.reshape(shape),
        col_gain.reshape(1, width),
        col_proj,
        col_gate_bias.reshape(1, width),
        col_out,
    )
    if splits > 1:
        updated = updated.reshape(full, cols, width)
        updated = lax.all_to_all(updated, "col", split_axis=0, concat_axis=1, tiled=True)
    return updated.reshape(local_rows, local_cols, width)


def solution(mesh):
    return jax.shard_map(
        per_device,
        mesh=mesh,
        in_specs=(P(("groups", "col"), "row", None), P(), P(), P(), P(), P(), P(), P(), P()),
        out_specs=P(("groups", "col"), "row", None),
        check_vma=False,
    )
```

```python
import functools
import math

import jax
import jax.numpy as jnp
from jax import lax
from jax.experimental import pallas as pl
from jax.experimental.pallas import tpu as pltpu
from jax.sharding import PartitionSpec as P

HEADS = 8
LANES = 128
F32 = jnp.float32
BF16 = jnp.bfloat16
MESH = pl.DeviceIdType.MESH


def ceil_to(value, step):
    return -(-value // step) * step


def nt(a, b):
    return lax.dot_general(a, b, (((1,), (1,)), ((), ())), preferred_element_type=F32)


def tn(a, b):
    return lax.dot_general(a, b, (((0,), (0,)), ((), ())), preferred_element_type=F32)


def nn(a, b):
    return jnp.dot(a, b, preferred_element_type=F32)


class Sizes:
    def __init__(self, width):
        self.width = width
        self.head = width // HEADS
        self.pad_head = ceil_to(self.head + 1, 16)
        self.pad_key = LANES // (LANES // self.head)
        while LANES % self.pad_key:
            self.pad_key += 1
        self.rows = HEADS * self.pad_head
        self.keys = HEADS * self.pad_key
        self.lanes = ceil_to(width, LANES)
        self.chunks = self.lanes // LANES

    def packed_shapes(self):
        return [
            ((self.keys, self.width), BF16),
            ((self.width, self.keys), BF16),
            ((self.rows, self.width), BF16),
            ((self.rows, self.width), BF16),
            ((self.rows, self.lanes), BF16),
            ((self.rows, 1), F32),
        ]

    def work_scratch(self, tokens, length):
        return [
            pltpu.VMEM((self.chunks, tokens, LANES), F32),
            pltpu.VMEM((self.chunks, tokens, LANES), F32),
            pltpu.VMEM((tokens, self.width), BF16),
            pltpu.VMEM((self.keys, tokens), BF16),
            pltpu.VMEM((tokens, self.keys), BF16),
            pltpu.VMEM((self.rows, tokens), BF16),
            pltpu.VMEM((self.rows, tokens), F32),
            pltpu.VMEM((2, length, HEADS * length), F32),
            pltpu.VMEM((2, length, HEADS * length), BF16),
            pltpu.VMEM((self.rows, tokens), BF16),
        ]


def prepare(sz, weights, packed):
    proj, bias, out = weights
    wqt, wk, wvt, wgt, wo, bias_col = packed

    def window(block):
        start = block * sz.width
        low = start // LANES * LANES
        high = min(ceil_to(start + sz.width, LANES), 4 * sz.width)
        return proj[:, low:high], start - low, high - low

    def hits(shape, axis, pad, shift):
        place = lax.broadcasted_iota(jnp.int32, shape, axis)
        source = lax.broadcasted_iota(jnp.int32, shape, 1 - axis) - shift
        inner = place % pad
        return (inner < sz.head) & (source == place // pad * sz.head + inner)

    def pick(*spec):
        return jnp.where(hits(*spec), 1.0, 0.0).astype(BF16)

    part, shift, size = window(1)
    wk[...] = nn(part, pick((size, sz.keys), 1, sz.pad_key, shift)).astype(BF16)
    for block, ref, pad in ((0, wqt, sz.pad_key), (2, wvt, sz.pad_head), (3, wgt, sz.pad_head)):
        part, shift, size = window(block)
        ref[...] = nt(pick((HEADS * pad, size), 0, pad, shift), part).astype(BF16)
    spec = (sz.rows, sz.width), 0, sz.pad_head, 0
    wo[...] = jnp.zeros(wo.shape, BF16)
    wo[:, : sz.width] = nn(pick(*spec), out[...]).astype(BF16)
    row = bias[...].reshape(1, sz.width)
    bias_col[...] = jnp.sum(jnp.where(hits(*spec), row, 0.0), axis=1, keepdims=True)


def attend(sz, groups, length, start_of, stride, per_group, gain, packed, work):
    wqt, wk, wvt, wgt, wo, bias_col = packed
    xs, ys, normed, queries, keys, values, gates, scores, weights, gated = work
    run = length // per_group
    factor = math.log2(math.e) / sz.head**0.5
    lane = lax.broadcasted_iota(jnp.int32, (1, sz.lanes), 1)
    inside = lane < sz.width
    gain_row = gain[...].reshape(1, sz.width)

    def places(group):
        return [pl.ds(start_of(group, c), run, stride=stride) for c in range(per_group)]

    def tokens_of(group):
        parts = [
            jnp.concatenate([xs[k, place, :] for place in places(group)], axis=0)
            for k in range(sz.chunks)
        ]
        return jnp.concatenate(parts, axis=1)

    for group in range(groups):
        x = tokens_of(group)
        mean = jnp.sum(x, axis=1, keepdims=True) * (1.0 / sz.width)
        centred = jnp.where(inside, x - mean, 0.0)
        spread = jnp.sum(centred * centred, axis=1, keepdims=True) * (1.0 / sz.width)
        value = centred[:, : sz.width] * lax.rsqrt(spread + 1e-05) * gain_row
        normed[group * length : (group + 1) * length] = value.astype(BF16)
    z = normed[...]
    feature = lax.broadcasted_iota(jnp.int32, (sz.rows, 1), 0)
    ones_row = jnp.where(feature % sz.pad_head == sz.head, 1.0, 0.0)
    queries[...] = (nt(wqt[...], z) * factor).astype(BF16)
    keys[...] = nn(z, wk[...]).astype(BF16)
    values[...] = (nt(wvt[...], z) + ones_row).astype(BF16)
    gates[...] = jax.nn.sigmoid(nt(wgt[...], z) + bias_col[...])
    pack = LANES // sz.pad_key
    zeros = jnp.zeros((sz.pad_key, length), BF16)

    def score(group):
        mine = slice(group * length, (group + 1) * length)
        for first in range(0, HEADS, pack):
            blocks = []
            for j in range(pack):
                low = (first + j) * sz.pad_key
                own = queries[low : low + sz.pad_key, mine]
                blocks.append(
                    jnp.concatenate([own if i == j else zeros for i in range(pack)], axis=1)
                )
            lanes = slice(first * sz.pad_key, (first + pack) * sz.pad_key)
            scores[group % 2, :, first * length : (first + pack) * length] = nn(
                keys[mine, lanes], jnp.concatenate(blocks, axis=0)
            )

    def soften(group):
        for head in range(HEADS):
            lanes = slice(head * length, (head + 1) * length)
            s = scores[group % 2, :, lanes]
            top = jnp.max(s, axis=0, keepdims=True)
            weights[group % 2, :, lanes] = jnp.exp2(s - top).astype(BF16)

    def mix(group):
        mine = slice(group * length, (group + 1) * length)
        for head in range(HEADS):
            rows = slice(head * sz.pad_head, (head + 1) * sz.pad_head)
            lanes = slice(head * length, (head + 1) * length)
            mixed = nn(values[rows, mine], weights[group % 2, :, lanes])
            total = mixed[sz.head : sz.head + 1]
            gated[rows, mine] = (mixed * (1.0 / total) * gates[rows, mine]).astype(BF16)

    score(0)
    for group in range(groups):
        if group + 1 < groups:
            score(group + 1)
        soften(group)
        mix(group)
    for group in range(groups):
        mine = slice(group * length, (group + 1) * length)
        y = tokens_of(group) + tn(gated[:, mine], wo[...])
        for k in range(sz.chunks):
            part = y[:, k * LANES : (k + 1) * LANES]
            for c, place in enumerate(places(group)):
                ys[k, place, :] = part[c * run : (c + 1) * run]


def spread_tokens(sz, source, xs):
    tokens = xs.shape[1]
    flat = source[...].astype(F32).reshape(tokens, sz.width)
    for k in range(sz.chunks):
        part = flat[:, k * LANES : min((k + 1) * LANES, sz.width)]
        if part.shape[1] < LANES:
            pad = jnp.zeros((tokens, LANES - part.shape[1]), F32)
            part = jnp.concatenate([part, pad], axis=1)
        xs[k] = part


def gather_tokens(sz, ys, target):
    shape = target.shape
    for k in range(sz.chunks):
        low, high = k * LANES, min((k + 1) * LANES, sz.width)
        part = ys[k][:, : high - low]
        target[..., low:high] = part.reshape(shape[:-1] + (high - low,)).astype(BF16)


def row_kernel(sz, n, rows, cols, *refs):
    x_ref, gain, *own_weights = refs[:5]
    next_weights = refs[5:8]
    result, *next_packed = refs[8:15]
    got, back, *rest = refs[15:]
    packed, rest = rest[:6], rest[6:]
    work = rest[:10]
    send_a, recv_a, send_b, recv_b, local_sem = rest[10:]
    me = lax.axis_index("row")
    block = rows * cols

    barrier = pltpu.get_barrier_semaphore()

    def greet(step, carry):
        peer = lax.rem(me + step, n)
        pl.semaphore_signal(barrier, inc=1, device_id={"row": peer}, device_id_type=MESH)
        return carry

    lax.fori_loop(1, n, greet, 0)
    pl.semaphore_wait(barrier, n - 1)

    def exchange(source, target, place, send, recv, body):
        def copy(peer, slot):
            return pltpu.make_async_remote_copy(
                src_ref=source.at[place(peer)],
                dst_ref=target.at[place(slot)],
                send_sem=send.at[peer],
                recv_sem=recv.at[slot],
                device_id={"row": peer},
                device_id_type=MESH,
            )

        def start(step, carry):
            copy(lax.rem(me + step, n), me).start()
            return carry

        lax.fori_loop(1, n, start, 0)
        own = pltpu.make_async_copy(source.at[place(me)], target.at[place(me)], local_sem)
        own.start()
        body()
        own.wait()

        def finish(step, carry):
            peer = lax.rem(me + step, n)
            copy(peer, me).wait_send()
            copy(peer, peer).wait_recv()
            return carry

        lax.fori_loop(1, n, finish, 0)

    exchange(
        x_ref,
        got,
        lambda device: pl.ds(device * rows, rows),
        send_a,
        recv_a,
        lambda: prepare(sz, own_weights, packed),
    )
    spread_tokens(sz, got, work[0])
    attend(
        sz, rows, n * cols, lambda g, c: g * cols + c, block, cols, gain, packed, work
    )
    gather_tokens(sz, work[1], back)
    exchange(
        back,
        result,
        lambda device: device,
        send_b,
        recv_b,
        lambda: prepare(sz, next_weights, next_packed),
    )


def col_kernel(sz, cols, x_ref, gain, *refs):
    packed, result, work = refs[:6], refs[6], refs[7:]
    spread_tokens(sz, x_ref, work[0])
    length = work[0].shape[1] // cols
    attend(sz, cols, length, lambda g, c: g, cols, 1, gain, packed, work)
    gather_tokens(sz, work[1], result)


VMEM = pl.BlockSpec(memory_space=pltpu.VMEM)


def per_device(
    pair_map, row_gain, row_proj, row_gate_bias, row_out, col_gain, col_proj, col_gate_bias, col_out
):
    local_rows, local_cols, width = pair_map.shape
    n = lax.axis_size("row")
    sz = Sizes(width)
    rows = local_rows // n
    tokens = local_rows * local_cols
    block = rows * local_cols
    shape = (n, block, width)
    done, *packed = pl.pallas_call(
        functools.partial(row_kernel, sz, n, rows, local_cols),
        out_shape=[jax.ShapeDtypeStruct(shape, BF16)]
        + [jax.ShapeDtypeStruct(*spec) for spec in sz.packed_shapes()],
        in_specs=[VMEM] * 8,
        out_specs=[VMEM] * 7,
        scratch_shapes=[pltpu.VMEM(pair_map.shape, BF16), pltpu.VMEM(shape, BF16)]
        + [pltpu.VMEM(*spec) for spec in sz.packed_shapes()]
        + sz.work_scratch(tokens, n * local_cols)
        + [pltpu.SemaphoreType.DMA((n,))] * 4
        + [pltpu.SemaphoreType.DMA],
        compiler_params=pltpu.CompilerParams(collective_id=0, has_side_effects=True),
        name="row_attention",
    )(pair_map, row_gain, row_proj, row_gate_bias, row_out, col_proj, col_gate_bias, col_out)
    splits = lax.axis_size("col")
    if splits > 1:
        done = done.reshape(local_rows, local_cols, width)
        done = lax.all_to_all(done, "col", split_axis=1, concat_axis=0, tiled=True)
        done = done.reshape(shape)
    cols = local_cols // splits
    full = tokens // cols
    updated = pl.pallas_call(
        functools.partial(col_kernel, sz, cols),
        out_shape=jax.ShapeDtypeStruct((full, cols, width), BF16),
        in_specs=[VMEM] * 8,
        out_specs=VMEM,
        scratch_shapes=sz.work_scratch(tokens, full),
        name="col_attention",
    )(done, col_gain, *packed)
    if splits > 1:
        updated = lax.all_to_all(updated, "col", split_axis=0, concat_axis=1, tiled=True)
    return updated


def solution(mesh):
    return jax.shard_map(
        per_device,
        mesh=mesh,
        in_specs=(P(("groups", "col"), "row", None), P(), P(), P(), P(), P(), P(), P(), P()),
        out_specs=P(("groups", "col"), "row", None),
        check_vma=False,
    )
```

```python
import functools
import math

import jax
import jax.numpy as jnp
from jax import lax
from jax.experimental import pallas as pl
from jax.experimental.pallas import tpu as pltpu
from jax.sharding import PartitionSpec as P

HEADS = 8
LANES = 128
F32 = jnp.float32
BF16 = jnp.bfloat16
MESH = pl.DeviceIdType.MESH


def ceil_to(value, step):
    return -(-value // step) * step


def nt(a, b):
    return lax.dot_general(a, b, (((1,), (1,)), ((), ())), preferred_element_type=F32)


def tn(a, b):
    return lax.dot_general(a, b, (((0,), (0,)), ((), ())), preferred_element_type=F32)


def nn(a, b):
    return jnp.dot(a, b, preferred_element_type=F32)


class Sizes:
    def __init__(self, width):
        self.width = width
        self.head = width // HEADS
        self.pad_head = ceil_to(self.head + 1, 16)
        self.pad_key = LANES // (LANES // self.head)
        while LANES % self.pad_key:
            self.pad_key += 1
        self.rows = HEADS * self.pad_head
        self.keys = HEADS * self.pad_key
        self.lanes = ceil_to(width, LANES)
        self.chunks = self.lanes // LANES
        self.full = width // LANES
        self.rest = width % LANES
        self.side = LANES // self.rest if self.rest else 1

    def packed_rows(self, block):
        assert self.rest == 0 or (LANES % self.rest == 0 and block % self.side == 0)
        return self.full * block + (block // self.side if self.rest else 0)

    def packed_shapes(self):
        return [
            ((self.keys, self.width), BF16),
            ((self.width, self.keys), BF16),
            ((self.rows, self.width), BF16),
            ((self.rows, self.width), BF16),
            ((self.rows, self.lanes), BF16),
            ((self.rows, 1), F32),
        ]

    def work_scratch(self, tokens, length):
        return [
            pltpu.VMEM((self.chunks, tokens, LANES), F32),
            pltpu.VMEM((self.chunks, tokens, LANES), F32),
            pltpu.VMEM((tokens, self.width), BF16),
            pltpu.VMEM((self.keys, tokens), BF16),
            pltpu.VMEM((tokens, self.keys), BF16),
            pltpu.VMEM((self.rows, tokens), BF16),
            pltpu.VMEM((self.rows, tokens), F32),
            pltpu.VMEM((2, length, HEADS * length), F32),
            pltpu.VMEM((2, length, HEADS * length), BF16),
            pltpu.VMEM((self.rows, tokens), BF16),
        ]


def prepare(sz, weights, packed):
    proj, bias, out = weights
    wqt, wk, wvt, wgt, wo, bias_col = packed

    def window(block):
        start = block * sz.width
        low = start // LANES * LANES
        high = min(ceil_to(start + sz.width, LANES), 4 * sz.width)
        return proj[:, low:high], start - low, high - low

    def hits(shape, axis, pad, shift):
        place = lax.broadcasted_iota(jnp.int32, shape, axis)
        source = lax.broadcasted_iota(jnp.int32, shape, 1 - axis) - shift
        inner = place % pad
        return (inner < sz.head) & (source == place // pad * sz.head + inner)

    def pick(*spec):
        return jnp.where(hits(*spec), 1.0, 0.0).astype(BF16)

    part, shift, size = window(1)
    wk[...] = nn(part, pick((size, sz.keys), 1, sz.pad_key, shift)).astype(BF16)
    for block, ref, pad in ((0, wqt, sz.pad_key), (2, wvt, sz.pad_head), (3, wgt, sz.pad_head)):
        part, shift, size = window(block)
        ref[...] = nt(pick((HEADS * pad, size), 0, pad, shift), part).astype(BF16)
    spec = (sz.rows, sz.width), 0, sz.pad_head, 0
    wo[...] = jnp.zeros(wo.shape, BF16)
    wo[:, : sz.width] = nn(pick(*spec), out[...]).astype(BF16)
    row = bias[...].reshape(1, sz.width)
    bias_col[...] = jnp.sum(jnp.where(hits(*spec), row, 0.0), axis=1, keepdims=True)


def attend(sz, groups, length, start_of, stride, per_group, gain, packed, work, emit=None):
    wqt, wk, wvt, wgt, wo, bias_col = packed
    xs, ys, normed, queries, keys, values, gates, scores, weights, gated = work
    run = length // per_group
    factor = math.log2(math.e) / sz.head**0.5
    lane = lax.broadcasted_iota(jnp.int32, (1, sz.lanes), 1)
    inside = lane < sz.width
    gain_row = gain[...].reshape(1, sz.width)

    def places(group):
        return [pl.ds(start_of(group, c), run, stride=stride) for c in range(per_group)]

    def tokens_of(group):
        parts = [
            jnp.concatenate([xs[k, place, :] for place in places(group)], axis=0)
            for k in range(sz.chunks)
        ]
        return jnp.concatenate(parts, axis=1)

    for group in range(groups):
        x = tokens_of(group)
        mean = jnp.sum(x, axis=1, keepdims=True) * (1.0 / sz.width)
        centred = jnp.where(inside, x - mean, 0.0)
        spread = jnp.sum(centred * centred, axis=1, keepdims=True) * (1.0 / sz.width)
        value = centred[:, : sz.width] * lax.rsqrt(spread + 1e-05) * gain_row
        normed[group * length : (group + 1) * length] = value.astype(BF16)
    z = normed[...]
    feature = lax.broadcasted_iota(jnp.int32, (sz.rows, 1), 0)
    ones_row = jnp.where(feature % sz.pad_head == sz.head, 1.0, 0.0)
    queries[...] = (nt(wqt[...], z) * factor).astype(BF16)
    keys[...] = nn(z, wk[...]).astype(BF16)
    values[...] = (nt(wvt[...], z) + ones_row).astype(BF16)
    gates[...] = jax.nn.sigmoid(nt(wgt[...], z) + bias_col[...])
    pack = LANES // sz.pad_key
    zeros = jnp.zeros((sz.pad_key, length), BF16)

    def score(group):
        mine = slice(group * length, (group + 1) * length)
        for first in range(0, HEADS, pack):
            blocks = []
            for j in range(pack):
                low = (first + j) * sz.pad_key
                own = queries[low : low + sz.pad_key, mine]
                blocks.append(
                    jnp.concatenate([own if i == j else zeros for i in range(pack)], axis=1)
                )
            lanes = slice(first * sz.pad_key, (first + pack) * sz.pad_key)
            scores[group % 2, :, first * length : (first + pack) * length] = nn(
                keys[mine, lanes], jnp.concatenate(blocks, axis=0)
            )

    def soften(group):
        for head in range(HEADS):
            lanes = slice(head * length, (head + 1) * length)
            s = scores[group % 2, :, lanes]
            top = jnp.max(s, axis=0, keepdims=True)
            weights[group % 2, :, lanes] = jnp.exp2(s - top).astype(BF16)

    def mix(group):
        mine = slice(group * length, (group + 1) * length)
        for head in range(HEADS):
            rows = slice(head * sz.pad_head, (head + 1) * sz.pad_head)
            lanes = slice(head * length, (head + 1) * length)
            mixed = nn(values[rows, mine], weights[group % 2, :, lanes])
            total = mixed[sz.head : sz.head + 1]
            gated[rows, mine] = (mixed * (1.0 / total) * gates[rows, mine]).astype(BF16)

    score(0)
    for group in range(groups):
        if group + 1 < groups:
            score(group + 1)
        soften(group)
        mix(group)
    for group in range(groups):
        mine = slice(group * length, (group + 1) * length)
        y = tokens_of(group) + tn(gated[:, mine], wo[...])
        if emit is not None:
            emit(group, y)
            continue
        for k in range(sz.chunks):
            part = y[:, k * LANES : (k + 1) * LANES]
            for c, place in enumerate(places(group)):
                ys[k, place, :] = part[c * run : (c + 1) * run]


def pack_tokens(sz, ys, target):
    tokens = ys.shape[1]
    n = target.shape[0]
    block = tokens // n
    for k in range(sz.full):
        part = ys[k].reshape(n, block, LANES)
        target[:, k * block : (k + 1) * block, :] = part.astype(BF16)
    if sz.rest:
        joined = None
        for q in range(sz.side):
            part = ys[sz.full, pl.ds(q, tokens // sz.side, stride=sz.side), :]
            part = pltpu.roll(part, q * sz.rest, 1) if q else part
            joined = part if joined is None else joined + part
        part = joined.reshape(n, block // sz.side, LANES)
        target[:, sz.full * block :, :] = part.astype(BF16)


def unpack_tokens(sz, source, xs):
    tokens = xs.shape[1]
    n = source.shape[0]
    block = tokens // n
    for k in range(sz.full):
        part = source[:, k * block : (k + 1) * block, :]
        xs[k] = part.astype(F32).reshape(tokens, LANES)
    if sz.rest:
        joined = source[:, sz.full * block :, :].astype(F32).reshape(tokens // sz.side, LANES)
        inside = lax.broadcasted_iota(jnp.int32, (1, LANES), 1) < sz.rest
        for q in range(sz.side):
            part = pltpu.roll(joined, LANES - q * sz.rest, 1) if q else joined
            place = pl.ds(q, tokens // sz.side, stride=sz.side)
            xs[sz.full, place, :] = jnp.where(inside, part, 0.0)


def turn_tokens(sz, n, rows, source, xs, ys):
    cols, width, length = source.shape
    for c in range(cols):
        turned = source[c].astype(F32).T
        for k in range(sz.chunks):
            part = turned[:, k * LANES : min((k + 1) * LANES, width)]
            if part.shape[1] < LANES:
                pad = jnp.zeros((length, LANES - part.shape[1]), F32)
                part = jnp.concatenate([part, pad], axis=1)
            xs[k, c * length : (c + 1) * length] = part
    for k in range(sz.chunks):
        for c in range(cols):
            for r in range(rows):
                part = xs[k, pl.ds(c * length + r, n, stride=rows), :]
                ys[k, pl.ds(r * cols + c, n, stride=rows * cols), :] = part


def row_kernel(sz, n, rows, cols, *refs):
    x_ref, gain, *own_weights = refs[:5]
    next_weights = refs[5:8]
    result, *next_packed = refs[8:15]
    sent, got, back, *rest = refs[15:]
    packed, rest = rest[:6], rest[6:]
    work = rest[:10]
    send_a, recv_a, send_b, recv_b, local_sem = rest[10:]
    me = lax.axis_index("row")
    block = rows * cols

    barrier = pltpu.get_barrier_semaphore()

    def greet(step, carry):
        peer = lax.rem(me + step, n)
        pl.semaphore_signal(barrier, inc=1, device_id={"row": peer}, device_id_type=MESH)
        return carry

    lax.fori_loop(1, n, greet, 0)
    turn_tokens(sz, n, rows, x_ref, work[0], work[1])
    pack_tokens(sz, work[1], sent)
    pl.semaphore_wait(barrier, n - 1)

    def exchange(source, target, send, recv, body):
        def copy(peer, slot):
            return pltpu.make_async_remote_copy(
                src_ref=source.at[peer],
                dst_ref=target.at[slot],
                send_sem=send.at[peer],
                recv_sem=recv.at[slot],
                device_id={"row": peer},
                device_id_type=MESH,
            )

        def start(step, carry):
            copy(lax.rem(me + step, n), me).start()
            return carry

        lax.fori_loop(1, n, start, 0)
        own = pltpu.make_async_copy(source.at[me], target.at[me], local_sem)
        own.start()
        body()
        own.wait()

        def finish(step, carry):
            peer = lax.rem(me + step, n)
            copy(peer, me).wait_send()
            copy(peer, peer).wait_recv()
            return carry

        lax.fori_loop(1, n, finish, 0)

    exchange(
        sent,
        got,
        send_a,
        recv_a,
        lambda: prepare(sz, own_weights, packed),
    )
    unpack_tokens(sz, got, work[0])
    attend(
        sz, rows, n * cols, lambda g, c: g * cols + c, block, cols, gain, packed, work
    )
    pack_tokens(sz, work[1], back)
    exchange(
        back,
        result,
        send_b,
        recv_b,
        lambda: prepare(sz, next_weights, next_packed),
    )


def col_kernel(sz, cols, x_ref, gain, *refs):
    packed, result, work = refs[:6], refs[6], refs[7:]
    unpack_tokens(sz, x_ref, work[0])
    length = work[0].shape[1] // cols

    def emit(group, y):
        result[group] = y[:, : sz.width].T.astype(BF16)

    attend(sz, cols, length, lambda g, c: g, cols, 1, gain, packed, work, emit)


def swap_columns(sz, done, block, rows, cols):
    n = done.shape[0]
    parts = [done[:, k * block : (k + 1) * block] for k in range(sz.full)]
    if sz.rest:
        parts.append(done[:, sz.full * block :].reshape(n, block, sz.rest))
    whole = jnp.concatenate(parts, -1).reshape(rows, cols, sz.width)
    whole = lax.all_to_all(whole, "col", split_axis=1, concat_axis=0, tiled=True)
    whole = whole.reshape(n, block, sz.width)
    parts = [whole[..., k * LANES : (k + 1) * LANES] for k in range(sz.full)]
    if sz.rest:
        parts.append(whole[..., sz.full * LANES :].reshape(n, block // sz.side, LANES))
    return jnp.concatenate(parts, 1)


VMEM = pl.BlockSpec(memory_space=pltpu.VMEM)


def per_device(
    pair_map, row_gain, row_proj, row_gate_bias, row_out, col_gain, col_proj, col_gate_bias, col_out
):
    local_rows, local_cols, width = pair_map.shape
    n = lax.axis_size("row")
    sz = Sizes(width)
    rows = local_rows // n
    tokens = local_rows * local_cols
    block = rows * local_cols
    shape = (n, sz.packed_rows(block), LANES)
    turned = jnp.transpose(pair_map, (1, 2, 0))
    done, *packed = pl.pallas_call(
        functools.partial(row_kernel, sz, n, rows, local_cols),
        out_shape=[jax.ShapeDtypeStruct(shape, BF16)]
        + [jax.ShapeDtypeStruct(*spec) for spec in sz.packed_shapes()],
        in_specs=[VMEM] * 8,
        out_specs=[VMEM] * 7,
        scratch_shapes=[pltpu.VMEM(shape, BF16)] * 3
        + [pltpu.VMEM(*spec) for spec in sz.packed_shapes()]
        + sz.work_scratch(tokens, n * local_cols)
        + [pltpu.SemaphoreType.DMA((n,))] * 4
        + [pltpu.SemaphoreType.DMA],
        compiler_params=pltpu.CompilerParams(collective_id=0, has_side_effects=True),
        name="row_attention",
    )(turned, row_gain, row_proj, row_gate_bias, row_out, col_proj, col_gate_bias, col_out)
    splits = lax.axis_size("col")
    if splits > 1:
        done = swap_columns(sz, done, block, local_rows, local_cols)
    cols = local_cols // splits
    full = tokens // cols
    updated = pl.pallas_call(
        functools.partial(col_kernel, sz, cols),
        out_shape=jax.ShapeDtypeStruct((cols, width, full), BF16),
        in_specs=[VMEM] * 8,
        out_specs=VMEM,
        scratch_shapes=sz.work_scratch(tokens, full),
        name="col_attention",
    )(done, col_gain, *packed)
    updated = jnp.transpose(updated, (2, 0, 1))
    if splits > 1:
        updated = lax.all_to_all(updated, "col", split_axis=0, concat_axis=1, tiled=True)
    return updated


def solution(mesh):
    return jax.shard_map(
        per_device,
        mesh=mesh,
        in_specs=(P(("groups", "col"), "row", None), P(), P(), P(), P(), P(), P(), P(), P()),
        out_specs=P(("groups", "col"), "row", None),
        check_vma=False,
    )
```

```python
import functools
import math

import jax
import jax.numpy as jnp
from jax import lax
from jax.experimental import pallas as pl
from jax.experimental.pallas import tpu as pltpu
from jax.sharding import PartitionSpec as P

HEADS = 8
LANES = 128
F32 = jnp.float32
BF16 = jnp.bfloat16
MESH = pl.DeviceIdType.MESH


def ceil_to(value, step):
    return -(-value // step) * step


def nt(a, b):
    return lax.dot_general(a, b, (((1,), (1,)), ((), ())), preferred_element_type=F32)


def tn(a, b):
    return lax.dot_general(a, b, (((0,), (0,)), ((), ())), preferred_element_type=F32)


def nn(a, b):
    return jnp.dot(a, b, preferred_element_type=F32)


class Sizes:
    def __init__(self, width):
        self.width = width
        self.head = width // HEADS
        self.pad_head = ceil_to(self.head + 1, 16)
        self.pad_key = LANES // (LANES // self.head)
        while LANES % self.pad_key:
            self.pad_key += 1
        self.rows = HEADS * self.pad_head
        self.keys = HEADS * self.pad_key
        self.lanes = ceil_to(width, LANES)
        self.chunks = self.lanes // LANES
        self.full = width // LANES
        self.rest = width % LANES
        self.side = LANES // self.rest if self.rest else 1

    def packed_rows(self, block):
        assert self.rest == 0 or (LANES % self.rest == 0 and block % self.side == 0)
        return self.full * block + (block // self.side if self.rest else 0)

    def packed_shapes(self):
        return [
            ((self.keys, self.width), BF16),
            ((self.width, self.keys), BF16),
            ((self.rows, self.width), BF16),
            ((self.rows, self.width), BF16),
            ((self.rows, self.lanes), BF16),
            ((self.rows, 1), F32),
        ]

    def work_scratch(self, tokens, length):
        return [
            pltpu.VMEM((self.chunks, tokens, LANES), F32),
            pltpu.VMEM((self.chunks, tokens, LANES), F32),
            pltpu.VMEM((tokens, self.width), BF16),
            pltpu.VMEM((self.keys, tokens), BF16),
            pltpu.VMEM((tokens, self.keys), BF16),
            pltpu.VMEM((self.rows, tokens), BF16),
            pltpu.VMEM((self.rows, tokens), F32),
            pltpu.VMEM((2, length, HEADS * length), F32),
            pltpu.VMEM((2, length, HEADS * length), BF16),
            pltpu.VMEM((self.rows, tokens), BF16),
        ]


def prepare(sz, weights, packed):
    proj, bias, out = weights
    wqt, wk, wvt, wgt, wo, bias_col = packed

    def window(block):
        start = block * sz.width
        low = start // LANES * LANES
        high = min(ceil_to(start + sz.width, LANES), 4 * sz.width)
        return proj[:, low:high], start - low, high - low

    def hits(shape, axis, pad, shift):
        place = lax.broadcasted_iota(jnp.int32, shape, axis)
        source = lax.broadcasted_iota(jnp.int32, shape, 1 - axis) - shift
        inner = place % pad
        return (inner < sz.head) & (source == place // pad * sz.head + inner)

    def pick(*spec):
        return jnp.where(hits(*spec), 1.0, 0.0).astype(BF16)

    part, shift, size = window(1)
    wk[...] = nn(part, pick((size, sz.keys), 1, sz.pad_key, shift)).astype(BF16)
    for block, ref, pad in ((0, wqt, sz.pad_key), (2, wvt, sz.pad_head), (3, wgt, sz.pad_head)):
        part, shift, size = window(block)
        ref[...] = nt(pick((HEADS * pad, size), 0, pad, shift), part).astype(BF16)
    spec = (sz.rows, sz.width), 0, sz.pad_head, 0
    wo[...] = jnp.zeros(wo.shape, BF16)
    wo[:, : sz.width] = nn(pick(*spec), out[...]).astype(BF16)
    row = bias[...].reshape(1, sz.width)
    bias_col[...] = jnp.sum(jnp.where(hits(*spec), row, 0.0), axis=1, keepdims=True)


def attend(sz, first, last, length, start_of, stride, per_group, gain, packed, work, emit=None):
    wqt, wk, wvt, wgt, wo, bias_col = packed
    xs, ys, normed, queries, keys, values, gates, scores, weights, gated = work
    run = length // per_group
    factor = math.log2(math.e) / sz.head**0.5
    lane = lax.broadcasted_iota(jnp.int32, (1, sz.lanes), 1)
    inside = lane < sz.width
    gain_row = gain[...].reshape(1, sz.width)

    def places(group):
        return [pl.ds(start_of(group, c), run, stride=stride) for c in range(per_group)]

    def tokens_of(group):
        parts = [
            jnp.concatenate([xs[k, place, :] for place in places(group)], axis=0)
            for k in range(sz.chunks)
        ]
        return jnp.concatenate(parts, axis=1)

    for group in range(first, last):
        x = tokens_of(group)
        mean = jnp.sum(x, axis=1, keepdims=True) * (1.0 / sz.width)
        centred = jnp.where(inside, x - mean, 0.0)
        spread = jnp.sum(centred * centred, axis=1, keepdims=True) * (1.0 / sz.width)
        value = centred[:, : sz.width] * lax.rsqrt(spread + 1e-05) * gain_row
        normed[group * length : (group + 1) * length] = value.astype(BF16)
    here = slice(first * length, last * length)
    z = normed[here]
    feature = lax.broadcasted_iota(jnp.int32, (sz.rows, 1), 0)
    ones_row = jnp.where(feature % sz.pad_head == sz.head, 1.0, 0.0)
    queries[:, here] = (nt(wqt[...], z) * factor).astype(BF16)
    keys[here] = nn(z, wk[...]).astype(BF16)
    values[:, here] = (nt(wvt[...], z) + ones_row).astype(BF16)
    gates[:, here] = jax.nn.sigmoid(nt(wgt[...], z) + bias_col[...])
    pack = LANES // sz.pad_key
    zeros = jnp.zeros((sz.pad_key, length), BF16)

    def score(group):
        mine = slice(group * length, (group + 1) * length)
        for start in range(0, HEADS, pack):
            blocks = []
            for j in range(pack):
                low = (start + j) * sz.pad_key
                own = queries[low : low + sz.pad_key, mine]
                blocks.append(
                    jnp.concatenate([own if i == j else zeros for i in range(pack)], axis=1)
                )
            lanes = slice(start * sz.pad_key, (start + pack) * sz.pad_key)
            scores[group % 2, :, start * length : (start + pack) * length] = nn(
                keys[mine, lanes], jnp.concatenate(blocks, axis=0)
            )

    def soften(group):
        for head in range(HEADS):
            lanes = slice(head * length, (head + 1) * length)
            s = scores[group % 2, :, lanes]
            top = jnp.max(s, axis=0, keepdims=True)
            weights[group % 2, :, lanes] = jnp.exp2(s - top).astype(BF16)

    def mix(group):
        mine = slice(group * length, (group + 1) * length)
        for head in range(HEADS):
            rows = slice(head * sz.pad_head, (head + 1) * sz.pad_head)
            lanes = slice(head * length, (head + 1) * length)
            mixed = nn(values[rows, mine], weights[group % 2, :, lanes])
            total = mixed[sz.head : sz.head + 1]
            gated[rows, mine] = (mixed * (1.0 / total) * gates[rows, mine]).astype(BF16)

    score(first)
    for group in range(first, last):
        if group + 1 < last:
            score(group + 1)
        soften(group)
        mix(group)
    for group in range(first, last):
        mine = slice(group * length, (group + 1) * length)
        y = tokens_of(group) + tn(gated[:, mine], wo[...])
        if emit is not None:
            emit(group, y)
            continue
        for k in range(sz.chunks):
            part = y[:, k * LANES : (k + 1) * LANES]
            for c, place in enumerate(places(group)):
                ys[k, place, :] = part[c * run : (c + 1) * run]


def pack_tokens(sz, ys, base, tokens, target):
    n = target.shape[0]
    block = tokens // n
    for k in range(sz.full):
        part = ys[k, base : base + tokens].reshape(n, block, LANES)
        target[:, k * block : (k + 1) * block, :] = part.astype(BF16)
    if sz.rest:
        joined = None
        for q in range(sz.side):
            part = ys[sz.full, pl.ds(base + q, tokens // sz.side, stride=sz.side), :]
            part = pltpu.roll(part, q * sz.rest, 1) if q else part
            joined = part if joined is None else joined + part
        part = joined.reshape(n, block // sz.side, LANES)
        target[:, sz.full * block :, :] = part.astype(BF16)


def unpack_tokens(sz, source, xs, base, tokens):
    n = source.shape[0]
    block = tokens // n
    for k in range(sz.full):
        part = source[:, k * block : (k + 1) * block, :]
        xs[k, base : base + tokens] = part.astype(F32).reshape(tokens, LANES)
    if sz.rest:
        joined = source[:, sz.full * block :, :].astype(F32).reshape(tokens // sz.side, LANES)
        inside = lax.broadcasted_iota(jnp.int32, (1, LANES), 1) < sz.rest
        for q in range(sz.side):
            part = pltpu.roll(joined, LANES - q * sz.rest, 1) if q else joined
            place = pl.ds(base + q, tokens // sz.side, stride=sz.side)
            xs[sz.full, place, :] = jnp.where(inside, part, 0.0)


def turn_tokens(sz, n, rows, span, source, xs, ys):
    cols, width, length = source.shape
    for c in range(cols):
        turned = source[c].astype(F32).T
        for k in range(sz.chunks):
            part = turned[:, k * LANES : min((k + 1) * LANES, width)]
            if part.shape[1] < LANES:
                pad = jnp.zeros((length, LANES - part.shape[1]), F32)
                part = jnp.concatenate([part, pad], axis=1)
            xs[k, c * length : (c + 1) * length] = part
    for k in range(sz.chunks):
        for c in range(cols):
            for r in range(rows):
                part = xs[k, pl.ds(c * length + r, n, stride=rows), :]
                first = r // span * n * span * cols + r % span * cols + c
                ys[k, pl.ds(first, n, stride=span * cols), :] = part


def row_chunks(rows, cols):
    return 2 if rows % 2 == 0 and rows // 2 * cols % 8 == 0 else 1


def row_kernel(sz, n, rows, cols, *refs):
    x_ref, gain, *own_weights = refs[:5]
    next_weights = refs[5:8]
    result, *next_packed = refs[8:15]
    sent, got, back, *rest = refs[15:]
    packed, rest = rest[:6], rest[6:]
    work = rest[:10]
    send_a, recv_a, send_b, recv_b, local_a, local_b = rest[10:]
    me = lax.axis_index("row")
    chunks = row_chunks(rows, cols)
    span = rows // chunks
    tokens = n * span * cols

    barrier = pltpu.get_barrier_semaphore()

    def greet(step, carry):
        peer = lax.rem(me + step, n)
        pl.semaphore_signal(barrier, inc=1, device_id={"row": peer}, device_id_type=MESH)
        return carry

    lax.fori_loop(1, n, greet, 0)
    turn_tokens(sz, n, rows, span, x_ref, work[0], work[1])
    for h in range(chunks):
        pack_tokens(sz, work[1], h * tokens, tokens, sent.at[h])
    pl.semaphore_wait(barrier, n - 1)

    def exchange(source, target, send, recv, local):
        def copy(peer, slot):
            return pltpu.make_async_remote_copy(
                src_ref=source.at[peer],
                dst_ref=target.at[slot],
                send_sem=send.at[peer],
                recv_sem=recv.at[slot],
                device_id={"row": peer},
                device_id_type=MESH,
            )

        own = pltpu.make_async_copy(source.at[me], target.at[me], local)

        def start():
            def step_on(step, carry):
                copy(lax.rem(me + step, n), me).start()
                return carry

            lax.fori_loop(1, n, step_on, 0)
            own.start()

        def arrive():
            def step_on(step, carry):
                peer = lax.rem(me + n - step, n)
                copy(peer, peer).wait_recv()
                return carry

            own.wait()
            lax.fori_loop(1, n, step_on, 0)

        def leave():
            def step_on(step, carry):
                copy(lax.rem(me + step, n), me).wait_send()
                return carry

            lax.fori_loop(1, n, step_on, 0)

        return start, arrive, leave

    there = [
        exchange(sent.at[h], got.at[h], send_a.at[h], recv_a.at[h], local_a.at[h])
        for h in range(chunks)
    ]
    home = [
        exchange(back.at[h], result.at[h], send_b.at[h], recv_b.at[h], local_b.at[h])
        for h in range(chunks)
    ]
    for start, _, _ in there:
        start()
    prepare(sz, own_weights, packed)
    for h in range(chunks):
        there[h][1]()
        unpack_tokens(sz, got.at[h], work[0], h * tokens, tokens)

        def start_of(group, c):
            return h * tokens + (group - h * span) * cols + c

        attend(
            sz,
            h * span,
            (h + 1) * span,
            n * cols,
            start_of,
            span * cols,
            cols,
            gain,
            packed,
            work,
        )
        pack_tokens(sz, work[1], h * tokens, tokens, back.at[h])
        home[h][0]()
    prepare(sz, next_weights, next_packed)
    for _, _, leave in there:
        leave()
    for _, arrive, leave in home:
        arrive()
        leave()


def col_kernel(sz, cols, rows, row_cols, x_ref, gain, *refs):
    packed, result, work = refs[:6], refs[6], refs[7:]
    xs, ys = work[:2]
    chunks, n = x_ref.shape[:2]
    tokens = xs.shape[1] // chunks
    span = rows // chunks
    landing = xs if chunks == 1 else ys
    for h in range(chunks):
        unpack_tokens(sz, x_ref.at[h], landing, h * tokens, tokens)
        if chunks == 1:
            continue
        for k in range(sz.chunks):
            for r in range(span):
                for c in range(row_cols):
                    part = ys[k, pl.ds(h * tokens + r * row_cols + c, n, stride=span * row_cols), :]
                    first = (h * span + r) * row_cols + c
                    xs[k, pl.ds(first, n, stride=rows * row_cols), :] = part
    length = xs.shape[1] // cols

    def emit(group, y):
        result[group] = y[:, : sz.width].T.astype(BF16)

    attend(sz, 0, cols, length, lambda g, c: g, cols, 1, gain, packed, work, emit)


def swap_columns(sz, done, rows, cols):
    chunks, n = done.shape[:2]
    span = rows // n // chunks
    block = span * cols
    done = jnp.swapaxes(done, 0, 1).reshape((chunks * n,) + done.shape[2:])
    parts = [done[:, k * block : (k + 1) * block] for k in range(sz.full)]
    if sz.rest:
        parts.append(done[:, sz.full * block :].reshape(chunks * n, block, sz.rest))
    whole = jnp.concatenate(parts, -1).reshape(rows, cols, sz.width)
    whole = lax.all_to_all(whole, "col", split_axis=1, concat_axis=0, tiled=True)
    block = rows * cols // n
    whole = whole.reshape(1, n, block, sz.width)
    parts = [whole[..., k * LANES : (k + 1) * LANES] for k in range(sz.full)]
    if sz.rest:
        parts.append(whole[..., sz.full * LANES :].reshape(1, n, block // sz.side, LANES))
    return jnp.concatenate(parts, 2)


VMEM = pl.BlockSpec(memory_space=pltpu.VMEM)


def per_device(
    pair_map, row_gain, row_proj, row_gate_bias, row_out, col_gain, col_proj, col_gate_bias, col_out
):
    local_rows, local_cols, width = pair_map.shape
    n = lax.axis_size("row")
    sz = Sizes(width)
    rows = local_rows // n
    tokens = local_rows * local_cols
    chunks = row_chunks(rows, local_cols)
    shape = (chunks, n, sz.packed_rows(rows // chunks * local_cols), LANES)
    turned = jnp.transpose(pair_map, (1, 2, 0))
    done, *packed = pl.pallas_call(
        functools.partial(row_kernel, sz, n, rows, local_cols),
        out_shape=[jax.ShapeDtypeStruct(shape, BF16)]
        + [jax.ShapeDtypeStruct(*spec) for spec in sz.packed_shapes()],
        in_specs=[VMEM] * 8,
        out_specs=[VMEM] * 7,
        scratch_shapes=[pltpu.VMEM(shape, BF16)] * 3
        + [pltpu.VMEM(*spec) for spec in sz.packed_shapes()]
        + sz.work_scratch(tokens, n * local_cols)
        + [pltpu.SemaphoreType.DMA((chunks, n))] * 4
        + [pltpu.SemaphoreType.DMA((chunks,))] * 2,
        compiler_params=pltpu.CompilerParams(collective_id=0, has_side_effects=True),
        name="row_attention",
    )(turned, row_gain, row_proj, row_gate_bias, row_out, col_proj, col_gate_bias, col_out)
    splits = lax.axis_size("col")
    if splits > 1:
        done = swap_columns(sz, done, local_rows, local_cols)
    cols = local_cols // splits
    full = tokens // cols
    updated = pl.pallas_call(
        functools.partial(col_kernel, sz, cols, rows, local_cols),
        out_shape=jax.ShapeDtypeStruct((cols, width, full), BF16),
        in_specs=[VMEM] * 8,
        out_specs=VMEM,
        scratch_shapes=sz.work_scratch(tokens, full),
        name="col_attention",
    )(done, col_gain, *packed)
    updated = jnp.transpose(updated, (2, 0, 1))
    if splits > 1:
        updated = lax.all_to_all(updated, "col", split_axis=0, concat_axis=1, tiled=True)
    return updated


def solution(mesh):
    return jax.shard_map(
        per_device,
        mesh=mesh,
        in_specs=(P(("groups", "col"), "row", None), P(), P(), P(), P(), P(), P(), P(), P()),
        out_specs=P(("groups", "col"), "row", None),
        check_vma=False,
    )
```

```python
import functools
import math

import jax
import jax.numpy as jnp
from jax import lax
from jax.experimental import pallas as pl
from jax.experimental.pallas import tpu as pltpu
from jax.sharding import PartitionSpec as P

HEADS = 8
LANES = 128
F32 = jnp.float32
BF16 = jnp.bfloat16
MESH = pl.DeviceIdType.MESH


def ceil_to(value, step):
    return -(-value // step) * step


def nt(a, b):
    return lax.dot_general(a, b, (((1,), (1,)), ((), ())), preferred_element_type=F32)


def tn(a, b):
    return lax.dot_general(a, b, (((0,), (0,)), ((), ())), preferred_element_type=F32)


def nn(a, b):
    return jnp.dot(a, b, preferred_element_type=F32)


class Sizes:
    def __init__(self, width):
        self.width = width
        self.head = width // HEADS
        self.pad_head = ceil_to(self.head + 1, 16)
        self.pad_key = LANES // (LANES // self.head)
        while LANES % self.pad_key:
            self.pad_key += 1
        self.rows = HEADS * self.pad_head
        self.keys = HEADS * self.pad_key
        self.lanes = ceil_to(width, LANES)
        self.chunks = self.lanes // LANES
        self.full = width // LANES
        self.rest = width % LANES
        self.side = LANES // self.rest if self.rest else 1

    def packed_rows(self, block):
        assert self.rest == 0 or (LANES % self.rest == 0 and block % self.side == 0)
        return self.full * block + (block // self.side if self.rest else 0)

    def packed_shapes(self):
        return [
            ((self.keys, self.width), BF16),
            ((self.width, self.keys), BF16),
            ((self.rows, self.width), BF16),
            ((self.rows, self.width), BF16),
            ((self.rows, self.lanes), BF16),
            ((self.rows, 1), F32),
        ]

    def work_scratch(self, tokens, length):
        return [
            pltpu.VMEM((self.chunks, tokens, LANES), F32),
            pltpu.VMEM((self.chunks, tokens, LANES), F32),
            pltpu.VMEM((tokens, self.width), BF16),
            pltpu.VMEM((self.keys, tokens), BF16),
            pltpu.VMEM((tokens, self.keys), BF16),
            pltpu.VMEM((self.rows, tokens), BF16),
            pltpu.VMEM((self.rows, tokens), F32),
            pltpu.VMEM((2, length, HEADS * length), F32),
            pltpu.VMEM((2, length, HEADS * length), BF16),
            pltpu.VMEM((self.rows, tokens), BF16),
        ]


def prepare(sz, weights, packed):
    proj, bias, out = weights
    wqt, wk, wvt, wgt, wo, bias_col = packed

    def window(block):
        start = block * sz.width
        low = start // LANES * LANES
        high = min(ceil_to(start + sz.width, LANES), 4 * sz.width)
        return proj[:, low:high], start - low, high - low

    def hits(shape, axis, pad, shift):
        place = lax.broadcasted_iota(jnp.int32, shape, axis)
        source = lax.broadcasted_iota(jnp.int32, shape, 1 - axis) - shift
        inner = place % pad
        return (inner < sz.head) & (source == place // pad * sz.head + inner)

    def pick(*spec):
        return jnp.where(hits(*spec), 1.0, 0.0).astype(BF16)

    part, shift, size = window(1)
    wk[...] = nn(part, pick((size, sz.keys), 1, sz.pad_key, shift)).astype(BF16)
    for block, ref, pad in ((0, wqt, sz.pad_key), (2, wvt, sz.pad_head), (3, wgt, sz.pad_head)):
        part, shift, size = window(block)
        ref[...] = nt(pick((HEADS * pad, size), 0, pad, shift), part).astype(BF16)
    spec = (sz.rows, sz.width), 0, sz.pad_head, 0
    wo[...] = jnp.zeros(wo.shape, BF16)
    wo[:, : sz.width] = nn(pick(*spec), out[...]).astype(BF16)
    row = bias[...].reshape(1, sz.width)
    bias_col[...] = jnp.sum(jnp.where(hits(*spec), row, 0.0), axis=1, keepdims=True)


def attend(sz, groups, length, start_of, stride, per_group, gain, packed, work, emit=None):
    wqt, wk, wvt, wgt, wo, bias_col = packed
    xs, ys, normed, queries, keys, values, gates, scores, weights, gated = work
    run = length // per_group
    factor = math.log2(math.e) / sz.head**0.5
    lane = lax.broadcasted_iota(jnp.int32, (1, sz.lanes), 1)
    inside = lane < sz.width
    gain_row = gain[...].reshape(1, sz.width)

    def places(group):
        return [pl.ds(start_of(group, c), run, stride=stride) for c in range(per_group)]

    def tokens_of(group):
        parts = [
            jnp.concatenate([xs[k, place, :] for place in places(group)], axis=0)
            for k in range(sz.chunks)
        ]
        return jnp.concatenate(parts, axis=1)

    for group in range(groups):
        x = tokens_of(group)
        mean = jnp.sum(x, axis=1, keepdims=True) * (1.0 / sz.width)
        centred = jnp.where(inside, x - mean, 0.0)
        spread = jnp.sum(centred * centred, axis=1, keepdims=True) * (1.0 / sz.width)
        value = centred[:, : sz.width] * lax.rsqrt(spread + 1e-05) * gain_row
        normed[group * length : (group + 1) * length] = value.astype(BF16)
    z = normed[...]
    feature = lax.broadcasted_iota(jnp.int32, (sz.rows, 1), 0)
    ones_row = jnp.where(feature % sz.pad_head == sz.head, 1.0, 0.0)
    queries[...] = (nt(wqt[...], z) * factor).astype(BF16)
    keys[...] = nn(z, wk[...]).astype(BF16)
    values[...] = (nt(wvt[...], z) + ones_row).astype(BF16)
    gates[...] = jax.nn.sigmoid(nt(wgt[...], z) + bias_col[...])
    pack = LANES // sz.pad_key
    zeros = jnp.zeros((sz.pad_key, length), BF16)

    def score(group):
        mine = slice(group * length, (group + 1) * length)
        for first in range(0, HEADS, pack):
            blocks = []
            for j in range(pack):
                low = (first + j) * sz.pad_key
                own = queries[low : low + sz.pad_key, mine]
                blocks.append(
                    jnp.concatenate([own if i == j else zeros for i in range(pack)], axis=1)
                )
            lanes = slice(first * sz.pad_key, (first + pack) * sz.pad_key)
            scores[group % 2, :, first * length : (first + pack) * length] = nn(
                keys[mine, lanes], jnp.concatenate(blocks, axis=0)
            )

    def soften(group):
        for head in range(HEADS):
            lanes = slice(head * length, (head + 1) * length)
            s = scores[group % 2, :, lanes]
            top = jnp.max(s, axis=0, keepdims=True)
            weights[group % 2, :, lanes] = jnp.exp2(s - top).astype(BF16)

    def mix(group):
        mine = slice(group * length, (group + 1) * length)
        for head in range(HEADS):
            rows = slice(head * sz.pad_head, (head + 1) * sz.pad_head)
            lanes = slice(head * length, (head + 1) * length)
            mixed = nn(values[rows, mine], weights[group % 2, :, lanes])
            total = mixed[sz.head : sz.head + 1]
            gated[rows, mine] = (mixed * (1.0 / total) * gates[rows, mine]).astype(BF16)

    score(0)
    for group in range(groups):
        if group + 1 < groups:
            score(group + 1)
        soften(group)
        mix(group)
    for group in range(groups):
        mine = slice(group * length, (group + 1) * length)
        y = tokens_of(group) + tn(gated[:, mine], wo[...])
        if emit is not None:
            emit(group, y)
            continue
        for k in range(sz.chunks):
            part = y[:, k * LANES : (k + 1) * LANES]
            for c, place in enumerate(places(group)):
                ys[k, place, :] = part[c * run : (c + 1) * run]


def pack_tokens(sz, ys, target):
    tokens = ys.shape[1]
    n = target.shape[0]
    block = tokens // n
    for k in range(sz.full):
        part = ys[k].reshape(n, block, LANES)
        target[:, k * block : (k + 1) * block, :] = part.astype(BF16)
    if sz.rest:
        joined = None
        for q in range(sz.side):
            part = ys[sz.full, pl.ds(q, tokens // sz.side, stride=sz.side), :]
            part = pltpu.roll(part, q * sz.rest, 1) if q else part
            joined = part if joined is None else joined + part
        part = joined.reshape(n, block // sz.side, LANES)
        target[:, sz.full * block :, :] = part.astype(BF16)


def unpack_tokens(sz, source, xs):
    tokens = xs.shape[1]
    n = source.shape[0]
    block = tokens // n
    for k in range(sz.full):
        part = source[:, k * block : (k + 1) * block, :]
        xs[k] = part.astype(F32).reshape(tokens, LANES)
    if sz.rest:
        joined = source[:, sz.full * block :, :].astype(F32).reshape(tokens // sz.side, LANES)
        inside = lax.broadcasted_iota(jnp.int32, (1, LANES), 1) < sz.rest
        for q in range(sz.side):
            part = pltpu.roll(joined, LANES - q * sz.rest, 1) if q else joined
            place = pl.ds(q, tokens // sz.side, stride=sz.side)
            xs[sz.full, place, :] = jnp.where(inside, part, 0.0)


def turn_tokens(sz, n, rows, source, xs, ys):
    cols, width, length = source.shape
    for c in range(cols):
        turned = source[c].astype(F32).T
        for k in range(sz.chunks):
            part = turned[:, k * LANES : min((k + 1) * LANES, width)]
            if part.shape[1] < LANES:
                pad = jnp.zeros((length, LANES - part.shape[1]), F32)
                part = jnp.concatenate([part, pad], axis=1)
            xs[k, c * length : (c + 1) * length] = part
    for k in range(sz.chunks):
        for c in range(cols):
            for r in range(rows):
                part = xs[k, pl.ds(c * length + r, n, stride=rows), :]
                ys[k, pl.ds(r * cols + c, n, stride=rows * cols), :] = part


def partners(me, n):
    if n & (n - 1):
        return [lax.rem(me + step, n) for step in range(1, n)]
    shifts = []
    weight = 1
    while weight < n:
        shifts.append(weight - 2 * weight * (me // weight % 2))
        weight *= 2
    flipped = {0: me}
    for step in range(1, n):
        high = step.bit_length() - 1
        flipped[step] = flipped[step - (1 << high)] + shifts[high]
    return [flipped[step] for step in range(n - 1, 0, -1)]


def row_kernel(sz, n, rows, cols, *refs):
    x_ref, gain, *own_weights = refs[:5]
    next_weights = refs[5:8]
    result, *next_packed = refs[8:15]
    sent, got, back, *rest = refs[15:]
    packed, rest = rest[:6], rest[6:]
    work = rest[:10]
    send_a, recv_a, send_b, recv_b, local_sem = rest[10:]
    me = lax.axis_index("row")
    block = rows * cols

    barrier = pltpu.get_barrier_semaphore()

    def greet(step, carry):
        peer = lax.rem(me + step, n)
        pl.semaphore_signal(barrier, inc=1, device_id={"row": peer}, device_id_type=MESH)
        return carry

    lax.fori_loop(1, n, greet, 0)
    turn_tokens(sz, n, rows, x_ref, work[0], work[1])
    pack_tokens(sz, work[1], sent)
    pl.semaphore_wait(barrier, n - 1)

    peers = partners(me, n)

    def exchange(source, target, send, recv, body):
        def copy(peer, slot):
            return pltpu.make_async_remote_copy(
                src_ref=source.at[peer],
                dst_ref=target.at[slot],
                send_sem=send.at[peer],
                recv_sem=recv.at[slot],
                device_id={"row": peer},
                device_id_type=MESH,
            )

        for peer in peers:
            copy(peer, me).start()
        own = pltpu.make_async_copy(source.at[me], target.at[me], local_sem)
        own.start()
        body()
        own.wait()

        def finish(step, carry):
            peer = lax.rem(me + step, n)
            copy(peer, me).wait_send()
            copy(peer, peer).wait_recv()
            return carry

        lax.fori_loop(1, n, finish, 0)

    exchange(
        sent,
        got,
        send_a,
        recv_a,
        lambda: prepare(sz, own_weights, packed),
    )
    unpack_tokens(sz, got, work[0])
    attend(
        sz, rows, n * cols, lambda g, c: g * cols + c, block, cols, gain, packed, work
    )
    pack_tokens(sz, work[1], back)
    exchange(
        back,
        result,
        send_b,
        recv_b,
        lambda: prepare(sz, next_weights, next_packed),
    )


def col_kernel(sz, cols, x_ref, gain, *refs):
    packed, result, work = refs[:6], refs[6], refs[7:]
    unpack_tokens(sz, x_ref, work[0])
    length = work[0].shape[1] // cols

    def emit(group, y):
        result[group] = y[:, : sz.width].T.astype(BF16)

    attend(sz, cols, length, lambda g, c: g, cols, 1, gain, packed, work, emit)


def swap_columns(sz, done, block, rows, cols):
    n = done.shape[0]
    parts = [done[:, k * block : (k + 1) * block] for k in range(sz.full)]
    if sz.rest:
        parts.append(done[:, sz.full * block :].reshape(n, block, sz.rest))
    whole = jnp.concatenate(parts, -1).reshape(rows, cols, sz.width)
    whole = lax.all_to_all(whole, "col", split_axis=1, concat_axis=0, tiled=True)
    whole = whole.reshape(n, block, sz.width)
    parts = [whole[..., k * LANES : (k + 1) * LANES] for k in range(sz.full)]
    if sz.rest:
        parts.append(whole[..., sz.full * LANES :].reshape(n, block // sz.side, LANES))
    return jnp.concatenate(parts, 1)


VMEM = pl.BlockSpec(memory_space=pltpu.VMEM)


def per_device(
    pair_map, row_gain, row_proj, row_gate_bias, row_out, col_gain, col_proj, col_gate_bias, col_out
):
    local_rows, local_cols, width = pair_map.shape
    n = lax.axis_size("row")
    sz = Sizes(width)
    rows = local_rows // n
    tokens = local_rows * local_cols
    block = rows * local_cols
    shape = (n, sz.packed_rows(block), LANES)
    turned = jnp.transpose(pair_map, (1, 2, 0))
    done, *packed = pl.pallas_call(
        functools.partial(row_kernel, sz, n, rows, local_cols),
        out_shape=[jax.ShapeDtypeStruct(shape, BF16)]
        + [jax.ShapeDtypeStruct(*spec) for spec in sz.packed_shapes()],
        in_specs=[VMEM] * 8,
        out_specs=[VMEM] * 7,
        scratch_shapes=[pltpu.VMEM(shape, BF16)] * 3
        + [pltpu.VMEM(*spec) for spec in sz.packed_shapes()]
        + sz.work_scratch(tokens, n * local_cols)
        + [pltpu.SemaphoreType.DMA((n,))] * 4
        + [pltpu.SemaphoreType.DMA],
        compiler_params=pltpu.CompilerParams(collective_id=0, has_side_effects=True),
        name="row_attention",
    )(turned, row_gain, row_proj, row_gate_bias, row_out, col_proj, col_gate_bias, col_out)
    splits = lax.axis_size("col")
    if splits > 1:
        done = swap_columns(sz, done, block, local_rows, local_cols)
    cols = local_cols // splits
    full = tokens // cols
    updated = pl.pallas_call(
        functools.partial(col_kernel, sz, cols),
        out_shape=jax.ShapeDtypeStruct((cols, width, full), BF16),
        in_specs=[VMEM] * 8,
        out_specs=VMEM,
        scratch_shapes=sz.work_scratch(tokens, full),
        name="col_attention",
    )(done, col_gain, *packed)
    updated = jnp.transpose(updated, (2, 0, 1))
    if splits > 1:
        updated = lax.all_to_all(updated, "col", split_axis=0, concat_axis=1, tiled=True)
    return updated


def solution(mesh):
    return jax.shard_map(
        per_device,
        mesh=mesh,
        in_specs=(P(("groups", "col"), "row", None), P(), P(), P(), P(), P(), P(), P(), P()),
        out_specs=P(("groups", "col"), "row", None),
        check_vma=False,
    )
```
